1024 devices in a mesh: half: 2 (over x_hi), ex: 16 (over z, core), fr: 32 (over x_lo, y).
Axes of the slice: x: 8 (x_hi: 2, x_lo: 4; x = x_hi * 4 + x_lo), y: 8, z: 8, core: 2. Of those that a mesh axis runs over, the one named last changes fastest.
Arguments:
- frame_patch_tokens: bfloat16 [2, 32, 32, 256, 1024], P('half', 'fr', 'ex'), may hold values from -12 to 12
- episode_first_frame: int32 [2, 1024], P('half'), may hold values from 0 to 1023, as said below
- router: bfloat16 [1024, 256], replicated, may hold values from -2 to 2
- expert_up_weight: bfloat16 [16, 1024, 2048], P('ex', None, 'half'), may hold values from -0.1875 to 0.1875
- expert_down_weight: bfloat16 [16, 2048, 1024], P('ex', 'half'), may hold values from -0.125 to 0.125
- query_key_value_weight: bfloat16 [1024, 1536], replicated, may hold values from -0.1875 to 0.1875
- head_score_scale: float32 [8], replicated, may hold values from 0.5 to 2
Outputs:
- attended: bfloat16 [2, 1024, 256, 512], P('half', 'fr', 'ex')
The draws below stay inside these ranges and needn't reach their ends.
Inputs may be any that keep to these rules, and one draw needn't show every extreme that they name: `episode_first_frame`: entry t of a sequence is the first frame of frame t's episode: at most t, equal to t or to entry t - 1, and 0 at t = 0; a new episode begins at the last frame.
All inputs are finite; a program needn't handle non-finite values.
Results may differ from the reference program's by a relative error of at most 0.0088.
Values may be sent and summed in bfloat16 or wider, within the bound.
A program may use at most 64 MiB of HBM per device.

```python
import math
import jax
import jax.numpy as jnp
from jax import lax

D = 1024
SPE = 2
HID = 2048
P_SIZE = 256
POLICY_HEADS = 8
HEAD_SIZE = 64
LOOK = 4
SPAN = 32
SEQ = 1024
SLOTS = 256
N_HALF = 2
N_EX = 16
N_FR = 32


def draw_frame_patch_tokens(key, part):
    full_shape = (N_HALF, N_FR, SPAN, P_SIZE, D)
    values = jax.random.normal(jax.random.fold_in(key, 1), full_shape, jnp.float32)
    return jnp.clip(values, -12.0, 12.0).astype(jnp.bfloat16)


def draw_router(key, part):
    entries = jax.random.normal(jax.random.fold_in(key, 11), (D, SLOTS), jnp.float32) * (3.0 / jnp.sqrt(jnp.float32(D)))
    values = entries
    clip_bound = 2048.0 / D
    return jnp.clip(values, -clip_bound, clip_bound).astype(jnp.bfloat16)


def draw_episode_first_frame(key, part):
    resets = jax.random.randint(jax.random.fold_in(key, 21), (N_HALF, SEQ), 0, 80) == 0
    forced_reset = jax.random.randint(jax.random.fold_in(key, 22), (N_HALF, 1), 1, SEQ - 1)
    frame_time = jnp.broadcast_to(jnp.arange(SEQ, dtype=jnp.int32), (N_HALF, SEQ))
    marked = jnp.where(resets | (frame_time == forced_reset) | (frame_time == 0) | (frame_time == SEQ - 1), frame_time, 0)
    return lax.cummax(marked, axis=1).astype(jnp.int32)


def level_of(own_key, extent, pieces, smallest, largest):
    level = 1.0
    for dim, blocks in pieces:
        draws = jax.random.uniform(jax.random.fold_in(jax.random.fold_in(own_key, 6), dim), (blocks,), jnp.float32, smallest / len(pieces), largest / len(pieces))
        level = level * jnp.repeat(jnp.exp(draws), extent[dim] // blocks).reshape((-1,) + (1,) * (len(extent) - 1 - dim))
    return level


def centred(stream_key, shape, deviation, most, cuts=(), held_as=jnp.bfloat16):
    level = level_of(stream_key, shape, cuts, -0.22, 0.18) if cuts else 1.0
    array = jax.random.normal(stream_key, shape, jnp.float32) * deviation * level
    return jnp.minimum(jnp.maximum(array, -most), most).astype(held_as)


def setup_inputs(seed: int = 0) -> dict:
    key_of = jax.random.split(jax.random.key(seed), 8)
    frame_patch_tokens = draw_frame_patch_tokens(jax.random.fold_in(key_of[7], 71), 0)
    episode_first_frame = draw_episode_first_frame(jax.random.fold_in(key_of[7], 71), 0)
    router = draw_router(jax.random.fold_in(key_of[7], 71), 0)
    expert_up_weight = centred(key_of[3], (N_EX, D, HID), D ** -0.5, 0.1875, ((0, 16), (2, 2)))
    expert_down_weight = centred(key_of[4], (N_EX, HID, D), HID ** -0.5, 0.125, ((0, 16), (1, 2)))
    query_key_value_weight = centred(key_of[5], (D, 3 * POLICY_HEADS * HEAD_SIZE), D ** -0.5, 0.1875)
    head_score_scale = jnp.clip(jnp.exp(jax.random.uniform(key_of[6], (POLICY_HEADS,), jnp.float32, math.log(0.5), math.log(2.0))), 0.5, 2.0)
    return {"frame_patch_tokens": frame_patch_tokens, "episode_first_frame": episode_first_frame, "router": router, "expert_up_weight": expert_up_weight, "expert_down_weight": expert_down_weight, "query_key_value_weight": query_key_value_weight, "head_score_scale": head_score_scale}


epsilon = 1e-06

def normalize_rows(values):
    return values * lax.rsqrt(lax.optimization_barrier(jnp.mean(values * values, axis=-1, keepdims=True)) + epsilon)

def widen(values):
    return lax.optimization_barrier(values.astype(jnp.bfloat16)).astype(jnp.float32)

def reference(frame_patch_tokens, episode_first_frame, router, expert_up_weight, expert_down_weight, query_key_value_weight, head_score_scale):
    window_slots = SPE * N_EX
    router_wide = router.astype(jnp.float32)
    up_wide = expert_up_weight.astype(jnp.float32)
    down_wide = expert_down_weight.astype(jnp.float32)
    blocks = frame_patch_tokens.reshape(N_HALF * N_FR, SPAN, P_SIZE, D)

    def encode(tokens):
        tokens_wide = tokens.astype(jnp.float32)
        scaled = widen(normalize_rows(tokens_wide))
        logits = jnp.einsum('fpd,ds->fps', scaled, router_wide)
        dispatch = widen(jax.nn.softmax(logits[:, :, :window_slots], axis=1))
        slot_data = widen(jnp.einsum('fps,fpd->fsd', dispatch, tokens_wide))
        combine = jax.nn.softmax(logits, axis=2)[:, :, :window_slots]
        grouped = slot_data.reshape(SPAN, N_EX, SPE, D)
        hidden = widen(jax.nn.gelu(jnp.einsum('fesd,edh->fesh', grouped, up_wide)))
        expert_result = jnp.einsum('fesh,ehd->fesd', hidden, down_wide).reshape(SPAN, window_slots, D)
        mixture = jnp.einsum('fps,fsd->fpd', combine, expert_result, precision=lax.Precision.HIGHEST)
        return normalize_rows(tokens_wide + mixture).astype(jnp.bfloat16)
    normed = lax.map(encode, blocks).reshape(N_HALF, SEQ, P_SIZE, D)
    frame_time = jnp.arange(SEQ, dtype=jnp.int32)
    later = frame_time[None, None, :]
    earlier = frame_time[None, :, None]
    allowed = (later <= earlier) & (later > earlier - LOOK * SPAN) & (later >= episode_first_frame[:, :, None])
    score_scale_factor = head_score_scale / math.sqrt(HEAD_SIZE)

    def policy(tokens):
        projected = jnp.dot(tokens.reshape(N_HALF * SEQ, D), query_key_value_weight, preferred_element_type=jnp.float32)
        projected = projected.reshape(N_HALF, SEQ, 3, POLICY_HEADS, HEAD_SIZE)
        queries = widen(normalize_rows(projected[:, :, 0]))
        keyed = widen(normalize_rows(projected[:, :, 1]))
        valued = widen(projected[:, :, 2])
        raw_scores = jnp.einsum('mthd,muhd->mhtu', queries, keyed)
        weight = jnp.where(allowed[:, None], jnp.exp(raw_scores * score_scale_factor[None, :, None, None]), 0.0)
        totals = lax.optimization_barrier(jnp.sum(weight, axis=3))
        rounded = widen(weight)
        summed = jnp.einsum('mhtu,muhd->mthd', rounded, valued)
        attended = summed / jnp.transpose(totals, (0, 2, 1))[..., None]
        return attended.reshape(N_HALF, SEQ, POLICY_HEADS * HEAD_SIZE).astype(jnp.bfloat16)
    results = lax.map(policy, jnp.transpose(normed, (2, 0, 1, 3)))
    return jnp.transpose(results, (1, 2, 0, 3))
```

```python
import functools
import math

import jax
import jax.numpy as jnp
from jax import lax
from jax.experimental import pallas as pl
from jax.experimental.pallas import tpu as pltpu
from jax.sharding import PartitionSpec as P

SPE = 2
HEAD_SIZE = 64
HEADS = 8
WIDTH = HEADS * HEAD_SIZE
NY = 8
WINDOW = 128
MESH = pl.DeviceIdType.MESH

epsilon = 1e-06


def normalize_rows(values):
    return values * lax.rsqrt(jnp.mean(values * values, axis=-1, keepdims=True) + epsilon)


def half_ex(n_ex):
    me = lax.axis_index("half") * n_ex + lax.axis_index("ex")
    return me, lambda g: {"half": g // n_ex, "ex": lax.rem(g, n_ex)}


def y_ex(n_ex):
    fr = lax.axis_index("fr")
    y = lax.rem(fr, NY)
    me = y * n_ex + lax.axis_index("ex")
    return me, lambda g: {"fr": fr - y + g // n_ex, "ex": lax.rem(g, n_ex)}


def y_only(n_ex):
    fr = lax.axis_index("fr")
    y = lax.rem(fr, NY)
    return y, lambda g: {"fr": fr - y + g}


def exchange_kernel(group, n_ex, n, stride, pick, x_ref, o_ref, ssem, rsem, lsem):
    me, device = group(n_ex)

    def peer(i):
        return lax.rem(me + i * stride, n)

    barrier = pltpu.get_barrier_semaphore()

    def greet(i, _):
        pl.semaphore_signal(barrier, inc=1, device_id=device(peer(i)), device_id_type=MESH)
        return 0

    lax.fori_loop(1, n, greet, 0)
    own = pltpu.make_async_copy(pick(x_ref, me), o_ref.at[me], lsem)
    own.start()
    pl.semaphore_wait(barrier, n - 1)

    def send(i, _):
        g = peer(i)
        pltpu.make_async_remote_copy(
            pick(x_ref, g), o_ref.at[me], ssem, rsem, device_id=device(g), device_id_type=MESH
        ).start()
        return 0

    lax.fori_loop(1, n, send, 0)
    own.wait()
    rest = o_ref.at[pl.ds(0, n - 1)]
    pltpu.make_async_copy(rest, rest, rsem).wait()
    pltpu.make_async_copy(rest, rest, ssem).wait()


def exchange(x, out_shape, group, n_ex, n, stride, pick, number):
    return pl.pallas_call(
        functools.partial(exchange_kernel, group, n_ex, n, stride, pick),
        out_shape=jax.ShapeDtypeStruct(out_shape, x.dtype),
        in_specs=[pl.BlockSpec(memory_space=pltpu.VMEM)],
        out_specs=pl.BlockSpec(memory_space=pltpu.VMEM),
        scratch_shapes=[pltpu.SemaphoreType.DMA] * 3,
        compiler_params=pltpu.CompilerParams(collective_id=number, has_side_effects=True),
        name=f"exchange_{number}",
    )(x)


def first_lanes(shape):
    lane = lax.broadcasted_iota(jnp.int32, shape, len(shape) - 1)
    return lax.rem(lane, 2 * HEAD_SIZE) < HEAD_SIZE


def normalize_heads(values, low):
    square = values * values
    low_sum = jnp.sum(jnp.where(low, square, 0.0), axis=-1, keepdims=True)
    high_sum = jnp.sum(jnp.where(low, 0.0, square), axis=-1, keepdims=True)
    scale = jnp.where(
        low,
        lax.rsqrt(low_sum * (1.0 / HEAD_SIZE) + epsilon),
        lax.rsqrt(high_sum * (1.0 / HEAD_SIZE) + epsilon),
    )
    return (values * scale).astype(jnp.bfloat16)


def project_kernel(x_ref, w_ref, q_ref, near_ref, far_ref):
    rows = x_ref.shape[1]
    pair = 2 * HEAD_SIZE
    low = first_lanes((rows, pair))
    half = rows // 2
    for c in range(3 * WIDTH // pair):
        part = jnp.dot(
            x_ref[0], w_ref[:, c * pair : (c + 1) * pair], preferred_element_type=jnp.float32
        )
        if c < 2 * WIDTH // pair:
            part = normalize_heads(part, low)
        else:
            part = part.astype(jnp.bfloat16)
        if c < WIDTH // pair:
            q_ref[0, :, c * pair : (c + 1) * pair] = part
        else:
            at = c * pair - WIDTH
            near_ref[0, :, at : at + pair] = part[:half]
            far_ref[0, :, at : at + pair] = part[half:]


def project(rows, weight):
    patches, frames, width = rows.shape
    half = frames // 2
    kv = jax.ShapeDtypeStruct((patches, half, 2 * WIDTH), jnp.bfloat16)
    return pl.pallas_call(
        project_kernel,
        grid=(patches,),
        out_shape=(jax.ShapeDtypeStruct((patches, frames, WIDTH), jnp.bfloat16), kv, kv),
        in_specs=[
            pl.BlockSpec((1, frames, width), lambda p: (p, 0, 0)),
            pl.BlockSpec(weight.shape, lambda p: (0, 0)),
        ],
        out_specs=(
            pl.BlockSpec((1, frames, WIDTH), lambda p: (p, 0, 0)),
            pl.BlockSpec((1, half, 2 * WIDTH), lambda p: (p, 0, 0)),
            pl.BlockSpec((1, half, 2 * WIDTH), lambda p: (p, 0, 0)),
        ),
        cost_estimate=pl.CostEstimate(
            flops=2 * patches * frames * width * 3 * WIDTH, bytes_accessed=6 << 20, transcendentals=0
        ),
        name="project",
    )(rows, weight)


def attend_kernel(scale_ref, start_ref, q_ref, before_ref, own_ref, o_ref):
    rows = q_ref.shape[1]
    pair = 2 * HEAD_SIZE
    low = first_lanes((rows, pair))
    query = lax.broadcasted_iota(jnp.int32, (rows, rows), 0)
    key = lax.broadcasted_iota(jnp.int32, (rows, rows), 1)
    start = start_ref[...]
    own_allowed = (key <= query) & (key >= start)
    before_allowed = (key > query) & (key - WINDOW >= start)
    contract = (((1,), (1,)), ((), ()))
    for c in range(WIDTH // pair):
        lanes = slice(c * pair, (c + 1) * pair)
        values = slice(WIDTH + c * pair, WIDTH + (c + 1) * pair)
        q = q_ref[0, :, lanes]
        outs = []
        for side in range(2):
            picked = jnp.where(low if side == 0 else ~low, q, jnp.zeros_like(q))
            factor = scale_ref[2 * c + side]
            total = None
            out = None
            for kv_ref, allowed in ((before_ref, before_allowed), (own_ref, own_allowed)):
                score = lax.dot_general(
                    picked, kv_ref[0, :, lanes], contract, preferred_element_type=jnp.float32
                )
                weight = jnp.where(allowed, jnp.exp(score * factor), 0.0)
                part_total = jnp.sum(weight, axis=-1, keepdims=True)
                part = jnp.dot(
                    weight.astype(jnp.bfloat16),
                    kv_ref[0, :, values],
                    preferred_element_type=jnp.float32,
                )
                total = part_total if total is None else total + part_total
                out = part if out is None else out + part
            outs.append(out / total)
        o_ref[0, :, lanes] = jnp.where(low, outs[0], outs[1]).astype(o_ref.dtype)


def attend(scale, start, queries, block, before, own):
    patches = queries.shape[0]
    kv_spec = pl.BlockSpec((1, WINDOW, 2 * WIDTH), lambda p: (p, 0, 0))
    return pl.pallas_call(
        attend_kernel,
        grid=(patches,),
        out_shape=jax.ShapeDtypeStruct((patches, WINDOW, WIDTH), jnp.bfloat16),
        in_specs=[
            pl.BlockSpec(memory_space=pltpu.SMEM),
            pl.BlockSpec((WINDOW, 1), lambda p: (0, 0)),
            pl.BlockSpec((1, WINDOW, WIDTH), lambda p: (p, block, 0)),
            kv_spec,
            kv_spec,
        ],
        out_specs=pl.BlockSpec((1, WINDOW, WIDTH), lambda p: (p, 0, 0)),
        cost_estimate=pl.CostEstimate(
            flops=patches * 8 * WINDOW * WINDOW * 8 * WINDOW,
            bytes_accessed=3 << 20,
            transcendentals=patches * HEADS * 2 * WINDOW * WINDOW,
        ),
        name=f"attend_{block}",
    )(scale, start, queries, before, own)


def local(
    frame_patch_tokens,
    episode_first_frame,
    router,
    expert_up_weight,
    expert_down_weight,
    query_key_value_weight,
    head_score_scale,
):
    tokens = frame_patch_tokens[0, 0]
    frame_count, patch_count, model_width = tokens.shape
    n_ex = lax.axis_size("ex")
    n_half = lax.axis_size("half")
    n_fr = lax.axis_size("fr")
    window_slots = SPE * n_ex
    tokens_wide = tokens.astype(jnp.float32)
    scaled = normalize_rows(tokens_wide).astype(jnp.bfloat16)
    logits = jnp.einsum("fpd,ds->fps", scaled, router, preferred_element_type=jnp.float32)
    dispatch = jax.nn.softmax(logits[:, :, :window_slots], axis=1).astype(jnp.bfloat16)
    slot_data = jnp.einsum(
        "fps,fpd->fsd", dispatch, tokens, preferred_element_type=jnp.float32
    ).astype(jnp.bfloat16)
    combine = jax.nn.softmax(logits, axis=2)[:, :, :window_slots]
    chunk = (frame_count * SPE, model_width)
    outgoing = slot_data.reshape(frame_count, n_ex, SPE, model_width).transpose(1, 0, 2, 3)
    outgoing = outgoing.reshape((n_ex,) + chunk)
    n = n_half * n_ex
    received = exchange(
        outgoing, (n,) + chunk, half_ex, n_ex, n, 13, lambda ref, g: ref.at[lax.rem(g, n_ex)], 0
    )
    hidden = jax.nn.gelu(
        jnp.dot(
            received.reshape(-1, model_width), expert_up_weight[0], preferred_element_type=jnp.float32
        )
    ).astype(jnp.bfloat16)
    partial_value = jnp.dot(hidden, expert_down_weight[0], preferred_element_type=jnp.float32)
    partial_value = partial_value.astype(jnp.bfloat16).reshape((n,) + chunk)
    returned = exchange(
        partial_value, (n,) + chunk, half_ex, n_ex, n, 13, lambda ref, g: ref.at[g], 1
    )
    results = returned.reshape(n_half, n_ex, frame_count, SPE, model_width).astype(jnp.float32)
    results = results.sum(axis=0)
    expert_result = results.transpose(1, 0, 2, 3).reshape(frame_count, window_slots, model_width)
    mixture = jnp.einsum("fps,fsd->fpd", combine, expert_result, precision=lax.Precision.HIGHEST)
    normed = normalize_rows(tokens_wide + mixture).astype(jnp.bfloat16)

    owners = NY * n_ex
    per = patch_count // owners
    span = n_ex * frame_count
    normed = normed.reshape(frame_count, n_ex, NY, per, model_width).transpose(2, 1, 0, 3, 4)
    normed = normed.reshape(owners, frame_count * per, model_width)
    rows = exchange(normed, normed.shape, y_ex, n_ex, owners, 37, lambda ref, g: ref.at[g], 2)
    rows = rows.reshape(NY * span, per, model_width).transpose(1, 0, 2)
    queries, near, far = project(rows, query_key_value_weight)
    route = [(i, i + NY) for i in range(n_fr - NY)]
    halo = lax.ppermute(far, "fr", route)
    base = (lax.axis_index("fr") // NY) * (NY * span)
    starts = lax.dynamic_slice_in_dim(episode_first_frame[0], base, NY * span) - base
    starts = starts[:, None]
    scale = head_score_scale / math.sqrt(HEAD_SIZE)
    late = attend(scale, starts[WINDOW:] - WINDOW, queries, 1, near, far)
    early = attend(scale, starts[:WINDOW], queries, 0, halo, near)
    attended = jnp.concatenate([early, late], axis=1).reshape(per, NY, span, WIDTH)
    back = exchange(
        attended, (NY, per, span, WIDTH), y_only, n_ex, NY, 1, lambda ref, g: ref.at[:, g], 3
    )
    return back.transpose(2, 0, 1, 3).reshape(1, span, NY * per, WIDTH)


def solution(mesh):
    placed = (
        P("half", "fr", "ex", None, None),
        P("half", None),
        P(),
        P("ex", None, "half"),
        P("ex", "half", None),
        P(),
        P(),
    )
    return jax.shard_map(
        local, mesh=mesh, in_specs=placed, out_specs=P("half", "fr", "ex", None), check_vma=False
    )
```

```python
import functools
import math

import jax
import jax.numpy as jnp
from jax import lax
from jax.experimental import pallas as pl
from jax.experimental.pallas import tpu as pltpu
from jax.sharding import PartitionSpec as P

SPE = 2
HEAD_SIZE = 64
HEADS = 8
WIDTH = HEADS * HEAD_SIZE
NY = 8
WINDOW = 128
MESH = pl.DeviceIdType.MESH

epsilon = 1e-06


def normalize_rows(values):
    return values * lax.rsqrt(jnp.mean(values * values, axis=-1, keepdims=True) + epsilon)


def half_ex(n_ex):
    me = lax.axis_index("half") * n_ex + lax.axis_index("ex")
    return me, lambda g: {"half": g // n_ex, "ex": lax.rem(g, n_ex)}


def y_ex(n_ex):
    fr = lax.axis_index("fr")
    y = lax.rem(fr, NY)
    me = y * n_ex + lax.axis_index("ex")
    return me, lambda g: {"fr": fr - y + g // n_ex, "ex": lax.rem(g, n_ex)}


def exchange_kernel(group, n_ex, n, stride, pick, x_ref, o_ref, ssem, rsem, lsem):
    me, device = group(n_ex)

    def peer(i):
        return lax.rem(me + i * stride, n)

    barrier = pltpu.get_barrier_semaphore()

    def greet(i, _):
        pl.semaphore_signal(barrier, inc=1, device_id=device(peer(i)), device_id_type=MESH)
        return 0

    lax.fori_loop(1, n, greet, 0)
    own = pltpu.make_async_copy(pick(x_ref, me), o_ref.at[me], lsem)
    own.start()
    pl.semaphore_wait(barrier, n - 1)

    def send(i, _):
        g = peer(i)
        pltpu.make_async_remote_copy(
            pick(x_ref, g), o_ref.at[me], ssem, rsem, device_id=device(g), device_id_type=MESH
        ).start()
        return 0

    lax.fori_loop(1, n, send, 0)
    own.wait()
    rest = o_ref.at[pl.ds(0, n - 1)]
    pltpu.make_async_copy(rest, rest, rsem).wait()
    pltpu.make_async_copy(rest, rest, ssem).wait()


def exchange(x, out_shape, group, n_ex, n, stride, pick, number):
    return pl.pallas_call(
        functools.partial(exchange_kernel, group, n_ex, n, stride, pick),
        out_shape=jax.ShapeDtypeStruct(out_shape, x.dtype),
        in_specs=[pl.BlockSpec(memory_space=pltpu.VMEM)],
        out_specs=pl.BlockSpec(memory_space=pltpu.VMEM),
        scratch_shapes=[pltpu.SemaphoreType.DMA] * 3,
        compiler_params=pltpu.CompilerParams(collective_id=number, has_side_effects=True),
        name=f"exchange_{number}",
    )(x)


def first_lanes(shape):
    lane = lax.broadcasted_iota(jnp.int32, shape, len(shape) - 1)
    return lax.rem(lane, 2 * HEAD_SIZE) < HEAD_SIZE


def normalize_heads(values, low):
    square = values * values
    low_sum = jnp.sum(jnp.where(low, square, 0.0), axis=-1, keepdims=True)
    high_sum = jnp.sum(jnp.where(low, 0.0, square), axis=-1, keepdims=True)
    scale = jnp.where(
        low,
        lax.rsqrt(low_sum * (1.0 / HEAD_SIZE) + epsilon),
        lax.rsqrt(high_sum * (1.0 / HEAD_SIZE) + epsilon),
    )
    return (values * scale).astype(jnp.bfloat16)


def attend_block(scale_ref, allowed, low, q, before, own, p, out_ref, y0):
    pair = 2 * HEAD_SIZE
    contract = (((1,), (1,)), ((), ()))
    for c in range(WIDTH // pair):
        lanes = slice(c * pair, (c + 1) * pair)
        values = slice(WIDTH + c * pair, WIDTH + (c + 1) * pair)
        queries = q(p, lanes)
        outs, scales = [], []
        for side in range(2):
            picked = jnp.where(low if side == 0 else ~low, queries, jnp.zeros_like(queries))
            factor = scale_ref[2 * c + side]
            total = None
            out = None
            for kv, mask in zip((before, own), allowed):
                score = lax.dot_general(
                    picked, kv(p, lanes), contract, preferred_element_type=jnp.float32
                )
                weight = jnp.where(mask, jnp.exp(score * factor), 0.0)
                part_total = jnp.sum(weight, axis=-1, keepdims=True)
                part = jnp.dot(
                    weight.astype(jnp.bfloat16), kv(p, values), preferred_element_type=jnp.float32
                )
                total = part_total if total is None else total + part_total
                out = part if out is None else out + part
            outs.append(out)
            scales.append(1.0 / total)
        result = jnp.where(low, outs[0], outs[1]) * jnp.where(low, scales[0], scales[1])
        result = result.astype(out_ref.dtype)
        span = out_ref.shape[2]
        for y in range(WINDOW // span):
            out_ref[p, y0 + y, :, lanes] = result[y * span : (y + 1) * span]


def tail_kernel(
    n_ex,
    scale_ref,
    start_ref,
    x_ref,
    w_hbm,
    o_ref,
    rows_ref,
    wide_ref,
    w_ref,
    q_ref,
    kv_ref,
    halo_ref,
    att_ref,
    load_sem,
    own_sem,
    send_sem,
    recv_sem,
    halo_send,
    halo_recv,
    back_send,
    back_recv,
    back_own,
):
    fr = lax.axis_index("fr")
    fx = fr // NY
    y = lax.rem(fr, NY)
    n = NY * n_ex
    n_x = lax.axis_size("fr") // NY
    me, device = y_ex(n_ex)
    after = {"fr": lax.rem(fx + 1, n_x) * NY + y}
    ahead = {"fr": lax.rem(fx + n_x - 1, n_x) * NY + y}
    load = pltpu.make_async_copy(w_hbm, w_ref, load_sem)
    load.start()

    def peer(i):
        return lax.rem(me + i * 37, n)

    barrier = pltpu.get_barrier_semaphore()

    def greet(i, _):
        pl.semaphore_signal(barrier, inc=1, device_id=device(peer(i)), device_id_type=MESH)
        return 0

    lax.fori_loop(1, n, greet, 0)
    pl.semaphore_signal(barrier, inc=1, device_id=after, device_id_type=MESH)
    pl.semaphore_signal(barrier, inc=1, device_id=ahead, device_id_type=MESH)

    def pairs(g):
        return x_ref.at[:, lax.rem(g, n_ex) * NY + g // n_ex]

    own = pltpu.make_async_copy(pairs(me), rows_ref.at[me], own_sem)
    own.start()
    pl.semaphore_wait(barrier, n + 1)

    def send(i, _):
        g = peer(i)
        pltpu.make_async_remote_copy(
            pairs(g), rows_ref.at[me], send_sem, recv_sem, device_id=device(g), device_id_type=MESH
        ).start()
        return 0

    lax.fori_loop(1, n, send, 0)
    own.wait()
    rest = rows_ref.at[pl.ds(0, n - 1)]
    pltpu.make_async_copy(rest, rest, recv_sem).wait()
    load.wait()

    frames = n * x_ref.shape[0]
    tiles = 16
    wide_ref[...] = rows_ref[...].reshape(frames * tiles, 128).astype(jnp.float32)
    pair = 2 * HEAD_SIZE
    low = first_lanes((frames, pair))
    patches = q_ref.shape[0]
    groups = tiles // patches
    inputs = []
    for p in range(patches):
        inputs.append(
            jnp.concatenate(
                [
                    wide_ref[pl.ds(p * groups + k, frames, stride=tiles), :].astype(jnp.bfloat16)
                    for k in range(groups)
                ],
                axis=1,
            )
        )
    copies = []
    for p in range(patches):
        for c in range(2 * WIDTH // 256):
            part = jnp.dot(
                inputs[p],
                w_ref[:, WIDTH + c * 256 : WIDTH + (c + 1) * 256],
                preferred_element_type=jnp.float32,
            )
            for s in range(2):
                piece = part[:, s * pair : (s + 1) * pair]
                at = c * 256 + s * pair
                if at < WIDTH:
                    piece = normalize_heads(piece, low)
                kv_ref[p, :, at : at + pair] = piece.astype(jnp.bfloat16)
        copy = pltpu.make_async_remote_copy(
            kv_ref.at[p, pl.ds(WINDOW, WINDOW)],
            halo_ref.at[p],
            halo_send.at[p],
            halo_recv.at[p],
            device_id=after,
            device_id_type=MESH,
        )
        copy.start()
        copies.append(copy)
    for p in range(patches):
        for c in range(WIDTH // 256):
            part = jnp.dot(
                inputs[p], w_ref[:, c * 256 : (c + 1) * 256], preferred_element_type=jnp.float32
            )
            for s in range(2):
                at = c * 256 + s * pair
                q_ref[p, :, at : at + pair] = normalize_heads(part[:, s * pair : (s + 1) * pair], low)

    query = lax.broadcasted_iota(jnp.int32, (WINDOW, WINDOW), 0)
    key = lax.broadcasted_iota(jnp.int32, (WINDOW, WINDOW), 1)
    low = first_lanes((WINDOW, pair))

    def masks(start):
        return (key > query) & (key - WINDOW >= start), (key <= query) & (key >= start)

    def give_back(first, last):
        for to in range(first, last):

            @pl.when(y != to)
            def _():
                pltpu.make_async_remote_copy(
                    att_ref.at[:, to],
                    o_ref.at[y],
                    back_send,
                    back_recv,
                    device_id={"fr": fr - y + to},
                    device_id_type=MESH,
                ).start()

    late = masks(start_ref[WINDOW:] - WINDOW)
    for p in range(patches):
        attend_block(
            scale_ref,
            late,
            low,
            lambda p, l: q_ref[p, WINDOW:, l],
            lambda p, l: kv_ref[p, :WINDOW, l],
            lambda p, l: kv_ref[p, WINDOW:, l],
            p,
            att_ref,
            NY // 2,
        )
    give_back(NY // 2, NY)
    early = masks(start_ref[:WINDOW])
    for p in range(patches):
        copies[p].wait()
        attend_block(
            scale_ref,
            early,
            low,
            lambda p, l: q_ref[p, :WINDOW, l],
            lambda p, l: halo_ref[p, :, l],
            lambda p, l: kv_ref[p, :WINDOW, l],
            p,
            att_ref,
            0,
        )
    give_back(0, NY // 2)
    mine = pltpu.make_async_copy(att_ref.at[:, y], o_ref.at[y], back_own)
    mine.start()
    mine.wait()
    pltpu.make_async_copy(rest, rest, send_sem).wait()
    back = o_ref.at[pl.ds(0, NY - 1)]
    pltpu.make_async_copy(back, back, back_recv).wait()
    pltpu.make_async_copy(back, back, back_send).wait()


def tail(x, weight, scale, starts, n_ex):
    frame_count = x.shape[0]
    n = NY * n_ex
    frames = n * frame_count
    patches = x.shape[2] * x.shape[3] // weight.shape[0]
    span = frames // NY
    vmem = pl.BlockSpec(memory_space=pltpu.VMEM)
    dma = pltpu.SemaphoreType.DMA
    return pl.pallas_call(
        functools.partial(tail_kernel, n_ex),
        out_shape=jax.ShapeDtypeStruct((NY, patches, span, WIDTH), jnp.bfloat16),
        in_specs=[
            pl.BlockSpec(memory_space=pltpu.SMEM),
            vmem,
            vmem,
            pl.BlockSpec(memory_space=pl.ANY),
        ],
        out_specs=vmem,
        scratch_shapes=[
            pltpu.VMEM((n, frame_count) + x.shape[2:], jnp.bfloat16),
            pltpu.VMEM((frames * x.shape[2], x.shape[3]), jnp.float32),
            pltpu.VMEM(weight.shape, jnp.bfloat16),
            pltpu.VMEM((patches, frames, WIDTH), jnp.bfloat16),
            pltpu.VMEM((patches, frames, 2 * WIDTH), jnp.bfloat16),
            pltpu.VMEM((patches, WINDOW, 2 * WIDTH), jnp.bfloat16),
            pltpu.VMEM((patches, NY, span, WIDTH), jnp.bfloat16),
            dma,
            dma,
            dma,
            dma,
            dma((patches,)),
            dma((patches,)),
            dma,
            dma,
            dma,
        ],
        compiler_params=pltpu.CompilerParams(collective_id=2, has_side_effects=True),
        name="tail",
    )(scale, starts, x, weight)


def local(
    frame_patch_tokens,
    episode_first_frame,
    router,
    expert_up_weight,
    expert_down_weight,
    query_key_value_weight,
    head_score_scale,
):
    tokens = frame_patch_tokens[0, 0]
    frame_count, patch_count, model_width = tokens.shape
    n_ex = lax.axis_size("ex")
    n_half = lax.axis_size("half")
    n_fr = lax.axis_size("fr")
    window_slots = SPE * n_ex
    tokens_wide = tokens.astype(jnp.float32)
    scaled = normalize_rows(tokens_wide).astype(jnp.bfloat16)
    logits = jnp.einsum("fpd,ds->fps", scaled, router, preferred_element_type=jnp.float32)
    dispatch = jax.nn.softmax(logits[:, :, :window_slots], axis=1).astype(jnp.bfloat16)
    slot_data = jnp.einsum(
        "fps,fpd->fsd", dispatch, tokens, preferred_element_type=jnp.float32
    ).astype(jnp.bfloat16)
    combine = jax.nn.softmax(logits, axis=2)[:, :, :window_slots]
    chunk = (frame_count * SPE, model_width)
    outgoing = slot_data.reshape(frame_count, n_ex, SPE, model_width).transpose(1, 0, 2, 3)
    outgoing = outgoing.reshape((n_ex,) + chunk)
    n = n_half * n_ex
    received = exchange(
        outgoing, (n,) + chunk, half_ex, n_ex, n, 13, lambda ref, g: ref.at[lax.rem(g, n_ex)], 0
    )
    hidden = jax.nn.gelu(
        jnp.dot(
            received.reshape(-1, model_width), expert_up_weight[0], preferred_element_type=jnp.float32
        )
    ).astype(jnp.bfloat16)
    partial_value = jnp.dot(hidden, expert_down_weight[0], preferred_element_type=jnp.float32)
    partial_value = partial_value.astype(jnp.bfloat16).reshape((n,) + chunk)
    returned = exchange(
        partial_value, (n,) + chunk, half_ex, n_ex, n, 13, lambda ref, g: ref.at[g], 1
    )
    results = returned.reshape(n_half, n_ex, frame_count, SPE, model_width).astype(jnp.float32)
    results = results.sum(axis=0)
    expert_result = results.transpose(1, 0, 2, 3).reshape(frame_count, window_slots, model_width)
    mixture = jnp.einsum("fps,fsd->fpd", combine, expert_result, precision=lax.Precision.HIGHEST)
    normed = normalize_rows(tokens_wide + mixture).astype(jnp.bfloat16)

    span = n_ex * frame_count
    per = patch_count // (NY * n_ex)
    tiles = model_width // 128
    normed = normed.reshape(frame_count, patch_count // per, per * tiles, 128)
    base = (lax.axis_index("fr") // NY) * (NY * span)
    starts = lax.dynamic_slice_in_dim(episode_first_frame[0], base, NY * span) - base
    scale = head_score_scale / math.sqrt(HEAD_SIZE)
    back = tail(normed, query_key_value_weight, scale, starts[:, None], n_ex)
    return back.transpose(2, 0, 1, 3).reshape(1, span, NY * per, WIDTH)


def solution(mesh):
    placed = (
        P("half", "fr", "ex", None, None),
        P("half", None),
        P(),
        P("ex", None, "half"),
        P("ex", "half", None),
        P(),
        P(),
    )
    return jax.shard_map(
        local, mesh=mesh, in_specs=placed, out_specs=P("half", "fr", "ex", None), check_vma=False
    )
```

```python
import functools
import math

import jax
import jax.numpy as jnp
from jax import lax
from jax.experimental import pallas as pl
from jax.experimental.pallas import tpu as pltpu
from jax.sharding import PartitionSpec as P

SPE = 2
HEAD_SIZE = 64
HEADS = 8
WIDTH = HEADS * HEAD_SIZE
NY = 8
WINDOW = 128
LANES = 128
MESH = pl.DeviceIdType.MESH

epsilon = 1e-06


def normalize_rows(values):
    return values * lax.rsqrt(jnp.mean(values * values, axis=-1, keepdims=True) + epsilon)


def first_lanes(shape):
    lane = lax.broadcasted_iota(jnp.int32, shape, len(shape) - 1)
    return lax.rem(lane, 2 * HEAD_SIZE) < HEAD_SIZE


def normalize_heads(values, low):
    square = values * values
    low_sum = jnp.sum(jnp.where(low, square, 0.0), axis=-1, keepdims=True)
    high_sum = jnp.sum(jnp.where(low, 0.0, square), axis=-1, keepdims=True)
    scale = jnp.where(
        low,
        lax.rsqrt(low_sum * (1.0 / HEAD_SIZE) + epsilon),
        lax.rsqrt(high_sum * (1.0 / HEAD_SIZE) + epsilon),
    )
    return (values * scale).astype(jnp.bfloat16)


def attend_block(scale_ref, allowed, low, q, before, own, p, out_ref, y0):
    pair = 2 * HEAD_SIZE
    contract = (((1,), (1,)), ((), ()))
    for c in range(WIDTH // pair):
        lanes = slice(c * pair, (c + 1) * pair)
        values = slice(WIDTH + c * pair, WIDTH + (c + 1) * pair)
        queries = q(p, lanes)
        outs, scales = [], []
        for side in range(2):
            picked = jnp.where(low if side == 0 else ~low, queries, jnp.zeros_like(queries))
            factor = scale_ref[2 * c + side] * (1.0 / math.sqrt(HEAD_SIZE))
            total = None
            out = None
            for kv, mask in zip((before, own), allowed):
                score = lax.dot_general(
                    picked, kv(p, lanes), contract, preferred_element_type=jnp.float32
                )
                weight = jnp.where(mask, jnp.exp(score * factor), 0.0)
                part_total = jnp.sum(weight, axis=-1, keepdims=True)
                part = jnp.dot(
                    weight.astype(jnp.bfloat16), kv(p, values), preferred_element_type=jnp.float32
                )
                total = part_total if total is None else total + part_total
                out = part if out is None else out + part
            outs.append(out)
            scales.append(1.0 / total)
        result = jnp.where(low, outs[0], outs[1]) * jnp.where(low, scales[0], scales[1])
        result = result.astype(out_ref.dtype)
        span = out_ref.shape[2]
        for y in range(WINDOW // span):
            out_ref[p, y0 + y, :, lanes] = result[y * span : (y + 1) * span]


def split(values):
    first = values.astype(jnp.bfloat16)
    rest = values - first.astype(jnp.float32)
    second = rest.astype(jnp.bfloat16)
    third = (rest - second.astype(jnp.float32)).astype(jnp.bfloat16)
    return first, second, third


def product(left, right):
    a, b, c = split(left)
    x, y, z = split(right)
    return jnp.dot(
        jnp.concatenate([a, a, b, b, a, c], axis=1),
        jnp.concatenate([x, y, x, y, z, x], axis=0),
        preferred_element_type=jnp.float32,
    )


def put_rows(wide_ref, first, values):
    rows, width = values.shape
    groups = width // LANES
    for k in range(groups):
        wide_ref[pl.ds(first + k, rows, stride=groups), :] = values[:, k * LANES : (k + 1) * LANES]


def take_rows(wide_ref, first, rows, stride, groups):
    return [wide_ref[pl.ds(first + k, rows, stride=stride), :] for k in range(groups)]


def whole_kernel(
    n_half,
    n_ex,
    scale_ref,
    start_ref,
    tok_ref,
    router_ref,
    up_hbm,
    down_hbm,
    w_hbm,
    o_ref,
    slot_ref,
    slots_in_ref,
    part_ref,
    parts_in_ref,
    combine_ref,
    x_ref,
    rows_ref,
    wide_ref,
    up_ref,
    down_ref,
    w_ref,
    q_ref,
    kv_ref,
    halo_ref,
    att_ref,
    load_sem,
    own_sem,
    slot_sem,
    part_sem,
    token_sem,
    halo_send,
    halo_recv,
    back_sem,
):
    half = lax.axis_index("half")
    ex = lax.axis_index("ex")
    fr = lax.axis_index("fr")
    fx = fr // NY
    y = lax.rem(fr, NY)
    n = NY * n_ex
    n_x = lax.axis_size("fr") // NY
    me = y * n_ex + ex
    n_he = n_half * n_ex
    me_he = half * n_ex + ex
    after = {"fr": lax.rem(fx + 1, n_x) * NY + y}
    ahead = {"fr": lax.rem(fx + n_x - 1, n_x) * NY + y}
    frame_count, patch_count, width = tok_ref.shape
    groups = width // LANES
    tiles = x_ref.shape[2]
    patches = tiles // groups

    def device(g):
        return {"fr": fr - y + g // n_ex, "ex": lax.rem(g, n_ex)}

    def peer(i):
        return lax.rem(me + i * 37, n)

    def device_he(g):
        return {"half": g // n_ex, "ex": lax.rem(g, n_ex)}

    def peer_he(i):
        return lax.rem(me_he + i * 13, n_he)

    loads = []
    for number, (source, target) in enumerate(
        ((up_hbm.at[0], up_ref), (down_hbm.at[0], down_ref), (w_hbm, w_ref))
    ):
        load = pltpu.make_async_copy(source, target, load_sem.at[number])
        load.start()
        loads.append(load)

    barrier = pltpu.get_barrier_semaphore()

    def greet(i, _):
        pl.semaphore_signal(barrier, inc=1, device_id=device(peer(i)), device_id_type=MESH)
        return 0

    def greet_other(i, _):
        other = {"half": lax.rem(half + 1, n_half), "ex": i}
        pl.semaphore_signal(barrier, inc=1, device_id=other, device_id_type=MESH)
        return 0

    lax.fori_loop(0, n_ex, greet_other, 0)
    lax.fori_loop(1, n, greet, 0)
    pl.semaphore_signal(barrier, inc=1, device_id=after, device_id_type=MESH)
    pl.semaphore_signal(barrier, inc=1, device_id=ahead, device_id_type=MESH)

    window_slots = SPE * n_ex
    for f in range(frame_count):
        wide = tok_ref[f].astype(jnp.float32)
        logits = jnp.dot(
            normalize_rows(wide).astype(jnp.bfloat16),
            router_ref[...],
            preferred_element_type=jnp.float32,
        )
        turned = jnp.transpose(logits[:, :LANES])[:window_slots]
        dispatch = jnp.exp(turned - jnp.max(turned, axis=1, keepdims=True))
        dispatch = dispatch / jnp.sum(dispatch, axis=1, keepdims=True)
        data = jnp.dot(
            dispatch.astype(jnp.bfloat16), tok_ref[f], preferred_element_type=jnp.float32
        )
        put_rows(wide_ref, f * window_slots * groups, data)
        slot_ref[f] = (
            wide_ref[f * window_slots * groups : (f + 1) * window_slots * groups]
            .astype(jnp.bfloat16)
            .reshape(slot_ref.shape[1:])
        )
        combine_ref[f] = logits

    mine = pltpu.make_async_copy(slot_ref.at[:, ex], slots_in_ref.at[me_he], own_sem.at[0])
    mine.start()
    pl.semaphore_wait(barrier, n - 1 + n_ex + 2)

    def send_slots(i, _):
        g = peer_he(i)
        pltpu.make_async_remote_copy(
            slot_ref.at[:, lax.rem(g, n_ex)],
            slots_in_ref.at[me_he],
            slot_sem.at[0],
            slot_sem.at[1],
            device_id=device_he(g),
            device_id_type=MESH,
        ).start()
        return 0

    lax.fori_loop(1, n_he, send_slots, 0)
    for f in range(frame_count):
        logits = combine_ref[f]
        combine = jnp.exp(logits - jnp.max(logits, axis=1, keepdims=True))
        combine = combine / jnp.sum(combine, axis=1, keepdims=True)
        combine_ref[f] = combine
    mine.wait()
    rest = slots_in_ref.at[pl.ds(0, n_he - 1)]
    pltpu.make_async_copy(rest, rest, slot_sem.at[1]).wait()
    loads[0].wait()
    loads[1].wait()
    rows = n_he * frame_count * SPE
    wide_ref[: rows * groups] = slots_in_ref[...].reshape(rows * groups, LANES).astype(jnp.float32)
    slot_rows = jnp.concatenate(take_rows(wide_ref, 0, rows, groups, groups), axis=1)
    hidden = jax.nn.gelu(
        jnp.dot(slot_rows.astype(jnp.bfloat16), up_ref[...], preferred_element_type=jnp.float32)
    ).astype(jnp.bfloat16)
    partial_value = jnp.dot(hidden, down_ref[...], preferred_element_type=jnp.float32)
    put_rows(wide_ref, 0, partial_value)
    part_ref[...] = wide_ref[: rows * groups].astype(jnp.bfloat16).reshape(part_ref.shape)
    mine = pltpu.make_async_copy(part_ref.at[me_he], parts_in_ref.at[me_he], own_sem.at[1])
    mine.start()

    def send_parts(i, _):
        g = peer_he(i)
        pltpu.make_async_remote_copy(
            part_ref.at[g],
            parts_in_ref.at[me_he],
            part_sem.at[0],
            part_sem.at[1],
            device_id=device_he(g),
            device_id_type=MESH,
        ).start()
        return 0

    lax.fori_loop(1, n_he, send_parts, 0)
    mine.wait()
    pltpu.make_async_copy(rest, rest, part_sem.at[1]).wait()

    pairs = patch_count // patches
    for f in range(frame_count):
        result = parts_in_ref[:n_ex, f].astype(jnp.float32)
        for h in range(1, n_half):
            result = result + parts_in_ref[h * n_ex : (h + 1) * n_ex, f].astype(jnp.float32)
        wide_ref[: window_slots * groups] = result.reshape(window_slots * groups, LANES)
        result = jnp.concatenate(take_rows(wide_ref, 0, window_slots, groups, groups), axis=1)
        mixture = product(combine_ref[f][:, :window_slots], result)
        normed = normalize_rows(tok_ref[f].astype(jnp.float32) + mixture)
        put_rows(wide_ref, 0, normed)
        x_ref[f] = (
            wide_ref[: patch_count * groups].astype(jnp.bfloat16).reshape(pairs, tiles, LANES)
        )
        mine = pltpu.make_async_copy(
            x_ref.at[f, ex * NY + y], rows_ref.at[me, f], own_sem.at[2 + f]
        )
        mine.start()

        def send_tokens(i, _):
            g = peer(i)
            pltpu.make_async_remote_copy(
                x_ref.at[f, lax.rem(g, n_ex) * NY + g // n_ex],
                rows_ref.at[me, f],
                token_sem.at[0],
                token_sem.at[1],
                device_id=device(g),
                device_id_type=MESH,
            ).start()
            return 0

        lax.fori_loop(1, n, send_tokens, 0)
        mine.wait()
    tokens_in = rows_ref.at[pl.ds(0, n - 1)]
    pltpu.make_async_copy(tokens_in, tokens_in, token_sem.at[1]).wait()
    loads[2].wait()

    frames = n * frame_count
    wide_ref[...] = rows_ref[...].reshape(frames * tiles, LANES).astype(jnp.float32)
    pair = 2 * HEAD_SIZE
    low = first_lanes((frames, pair))
    inputs = []
    for p in range(patches):
        inputs.append(
            jnp.concatenate(
                [
                    piece.astype(jnp.bfloat16)
                    for piece in take_rows(wide_ref, p * groups, frames, tiles, groups)
                ],
                axis=1,
            )
        )
    copies = []
    for p in range(patches):
        for c in range(2 * WIDTH // 256):
            part = jnp.dot(
                inputs[p],
                w_ref[:, WIDTH + c * 256 : WIDTH + (c + 1) * 256],
                preferred_element_type=jnp.float32,
            )
            for s in range(2):
                piece = part[:, s * pair : (s + 1) * pair]
                at = c * 256 + s * pair
                if at < WIDTH:
                    piece = normalize_heads(piece, low)
                kv_ref[p, :, at : at + pair] = piece.astype(jnp.bfloat16)
        copy = pltpu.make_async_remote_copy(
            kv_ref.at[p, pl.ds(WINDOW, WINDOW)],
            halo_ref.at[p],
            halo_send.at[p],
            halo_recv.at[p],
            device_id=after,
            device_id_type=MESH,
        )
        copy.start()
        copies.append(copy)
    for p in range(patches):
        for c in range(WIDTH // 256):
            part = jnp.dot(
                inputs[p], w_ref[:, c * 256 : (c + 1) * 256], preferred_element_type=jnp.float32
            )
            for s in range(2):
                at = c * 256 + s * pair
                q_ref[p, :, at : at + pair] = normalize_heads(part[:, s * pair : (s + 1) * pair], low)

    query = lax.broadcasted_iota(jnp.int32, (WINDOW, WINDOW), 0)
    key = lax.broadcasted_iota(jnp.int32, (WINDOW, WINDOW), 1)
    low = first_lanes((WINDOW, pair))

    def masks(block):
        start = start_ref[pl.ds(fx * 2 + block, 1), :] - (fx * 2 + block) * WINDOW
        start = jnp.transpose(jnp.broadcast_to(start, (WINDOW, WINDOW)))
        return (key > query) & (key - WINDOW >= start), (key <= query) & (key >= start)

    def give_back(first, last):
        for to in range(first, last):

            @pl.when(y != to)
            def _():
                pltpu.make_async_remote_copy(
                    att_ref.at[:, to],
                    o_ref.at[y],
                    back_sem.at[0],
                    back_sem.at[1],
                    device_id={"fr": fr - y + to},
                    device_id_type=MESH,
                ).start()

    late = masks(1)
    for p in range(patches):
        attend_block(
            scale_ref,
            late,
            low,
            lambda p, l: q_ref[p, WINDOW:, l],
            lambda p, l: kv_ref[p, :WINDOW, l],
            lambda p, l: kv_ref[p, WINDOW:, l],
            p,
            att_ref,
            NY // 2,
        )
    give_back(NY // 2, NY)
    early = masks(0)
    for p in range(patches):
        copies[p].wait()
        attend_block(
            scale_ref,
            early,
            low,
            lambda p, l: q_ref[p, :WINDOW, l],
            lambda p, l: halo_ref[p, :, l],
            lambda p, l: kv_ref[p, :WINDOW, l],
            p,
            att_ref,
            0,
        )
    give_back(0, NY // 2)
    mine = pltpu.make_async_copy(att_ref.at[:, y], o_ref.at[y], own_sem.at[2 + frame_count])
    mine.start()
    mine.wait()
    pltpu.make_async_copy(rest, rest, slot_sem.at[0]).wait()
    pltpu.make_async_copy(rest, rest, part_sem.at[0]).wait()
    pltpu.make_async_copy(tokens_in, tokens_in, token_sem.at[0]).wait()
    back = o_ref.at[pl.ds(0, NY - 1)]
    pltpu.make_async_copy(back, back, back_sem.at[1]).wait()
    pltpu.make_async_copy(back, back, back_sem.at[0]).wait()


def local(
    frame_patch_tokens,
    episode_first_frame,
    router,
    expert_up_weight,
    expert_down_weight,
    query_key_value_weight,
    head_score_scale,
):
    tokens = frame_patch_tokens[0, 0]
    frame_count, patch_count, width = tokens.shape
    n_ex = lax.axis_size("ex")
    n_half = lax.axis_size("half")
    n_he = n_half * n_ex
    n = NY * n_ex
    frames = n * frame_count
    span = frames // NY
    patches = patch_count // n
    groups = width // LANES
    slots = SPE * n_ex
    hidden = expert_up_weight.shape[2]
    starts = episode_first_frame.reshape(-1, WINDOW)
    vmem = pl.BlockSpec(memory_space=pltpu.VMEM)
    hbm = pl.BlockSpec(memory_space=pl.ANY)
    dma = pltpu.SemaphoreType.DMA

    def held(*shape):
        return pltpu.VMEM(shape, jnp.bfloat16)

    back = pl.pallas_call(
        functools.partial(whole_kernel, n_half, n_ex),
        out_shape=jax.ShapeDtypeStruct((NY, patches, span, WIDTH), jnp.bfloat16),
        in_specs=[pl.BlockSpec(memory_space=pltpu.SMEM), vmem, vmem, vmem, hbm, hbm, hbm],
        out_specs=vmem,
        scratch_shapes=[
            held(frame_count, n_ex, SPE * groups, LANES),
            held(n_he, frame_count, SPE * groups, LANES),
            held(n_he, frame_count, SPE * groups, LANES),
            held(n_he, frame_count, SPE * groups, LANES),
            pltpu.VMEM((frame_count, patch_count, router.shape[1]), jnp.float32),
            held(frame_count, n, patches * groups, LANES),
            held(n, frame_count, patches * groups, LANES),
            pltpu.VMEM((frames * patches * groups, LANES), jnp.float32),
            held(width, hidden),
            held(hidden, width),
            held(*query_key_value_weight.shape),
            held(patches, frames, WIDTH),
            held(patches, frames, 2 * WIDTH),
            held(patches, WINDOW, 2 * WIDTH),
            held(patches, NY, span, WIDTH),
            dma((3,)),
            dma((3 + frame_count,)),
            dma((2,)),
            dma((2,)),
            dma((2,)),
            dma((patches,)),
            dma((patches,)),
            dma((2,)),
        ],
        compiler_params=pltpu.CompilerParams(collective_id=0, has_side_effects=True),
        name="whole",
    )(
        head_score_scale,
        starts,
        tokens,
        router,
        expert_up_weight,
        expert_down_weight,
        query_key_value_weight,
    )
    return back.transpose(2, 0, 1, 3).reshape(1, span, NY * patches, WIDTH)


def solution(mesh):
    placed = (
        P("half", "fr", "ex", None, None),
        P("half", None),
        P(),
        P("ex", None, "half"),
        P("ex", "half", None),
        P(),
        P(),
    )
    return jax.shard_map(
        local, mesh=mesh, in_specs=placed, out_specs=P("half", "fr", "ex", None), check_vma=False
    )
```

```python
import functools
import math

import jax
import jax.numpy as jnp
from jax import lax
from jax.experimental import pallas as pl
from jax.experimental.pallas import tpu as pltpu
from jax.sharding import PartitionSpec as P

SPE = 2
HEAD_SIZE = 64
HEADS = 8
WIDTH = HEADS * HEAD_SIZE
NY = 8
WINDOW = 128
LANES = 128
MESH = pl.DeviceIdType.MESH

epsilon = 1e-06


def normalize_rows(values):
    return values * lax.rsqrt(jnp.mean(values * values, axis=-1, keepdims=True) + epsilon)


def first_lanes(shape):
    lane = lax.broadcasted_iota(jnp.int32, shape, len(shape) - 1)
    return lax.rem(lane, 2 * HEAD_SIZE) < HEAD_SIZE


def normalize_heads(values, low):
    square = values * values
    low_sum = jnp.sum(jnp.where(low, square, 0.0), axis=-1, keepdims=True)
    high_sum = jnp.sum(jnp.where(low, 0.0, square), axis=-1, keepdims=True)
    scale = jnp.where(
        low,
        lax.rsqrt(low_sum * (1.0 / HEAD_SIZE) + epsilon),
        lax.rsqrt(high_sum * (1.0 / HEAD_SIZE) + epsilon),
    )
    return (values * scale).astype(jnp.bfloat16)


def attend_block(scale_ref, allowed, low, q, before, own, p, out_ref, y0):
    pair = 2 * HEAD_SIZE
    contract = (((1,), (1,)), ((), ()))
    for c in range(WIDTH // pair):
        lanes = slice(c * pair, (c + 1) * pair)
        values = slice(WIDTH + c * pair, WIDTH + (c + 1) * pair)
        queries = q(p, lanes)
        outs, scales = [], []
        for side in range(2):
            picked = jnp.where(low if side == 0 else ~low, queries, jnp.zeros_like(queries))
            factor = scale_ref[2 * c + side] * (1.0 / math.sqrt(HEAD_SIZE))
            total = None
            out = None
            for kv, mask in zip((before, own), allowed):
                score = lax.dot_general(
                    picked, kv(p, lanes), contract, preferred_element_type=jnp.float32
                )
                weight = jnp.where(mask, jnp.exp(score * factor), 0.0)
                part_total = jnp.sum(weight, axis=-1, keepdims=True)
                part = jnp.dot(
                    weight.astype(jnp.bfloat16), kv(p, values), preferred_element_type=jnp.float32
                )
                total = part_total if total is None else total + part_total
                out = part if out is None else out + part
            outs.append(out)
            scales.append(1.0 / total)
        result = jnp.where(low, outs[0], outs[1]) * jnp.where(low, scales[0], scales[1])
        result = result.astype(out_ref.dtype)
        span = out_ref.shape[2]
        for y in range(WINDOW // span):
            out_ref[p, y0 + y, :, lanes] = result[y * span : (y + 1) * span]


def split(values):
    first = values.astype(jnp.bfloat16)
    rest = values - first.astype(jnp.float32)
    second = rest.astype(jnp.bfloat16)
    third = (rest - second.astype(jnp.float32)).astype(jnp.bfloat16)
    return first, second, third


def product(left, right):
    a, b, c = split(left)
    x, y, z = split(right)
    return jnp.dot(
        jnp.concatenate([a, a, b, b, a, c], axis=1),
        jnp.concatenate([x, y, x, y, z, x], axis=0),
        preferred_element_type=jnp.float32,
    )


def put_rows(wide_ref, first, values):
    rows, width = values.shape
    groups = width // LANES
    for k in range(groups):
        wide_ref[pl.ds(first + k, rows, stride=groups), :] = values[:, k * LANES : (k + 1) * LANES]


def take_rows(wide_ref, first, rows, stride, groups):
    return [wide_ref[pl.ds(first + k, rows, stride=stride), :] for k in range(groups)]


def whole_kernel(
    n_half,
    n_ex,
    scale_ref,
    start_ref,
    tok_ref,
    router_ref,
    up_hbm,
    down_hbm,
    w_hbm,
    o_ref,
    slot_ref,
    slots_in_ref,
    part_ref,
    parts_in_ref,
    combine_ref,
    x_ref,
    rows_ref,
    wide_ref,
    up_ref,
    down_ref,
    w_ref,
    q_ref,
    kv_ref,
    halo_ref,
    att_ref,
    load_sem,
    own_sem,
    slot_sem,
    part_sem,
    token_send,
    token_recv,
    halo_send,
    halo_recv,
    back_sem,
):
    half = lax.axis_index("half")
    ex = lax.axis_index("ex")
    fr = lax.axis_index("fr")
    fx = fr // NY
    y = lax.rem(fr, NY)
    n = NY * n_ex
    n_x = lax.axis_size("fr") // NY
    me = y * n_ex + ex
    n_he = n_half * n_ex
    me_he = half * n_ex + ex
    after = {"fr": lax.rem(fx + 1, n_x) * NY + y}
    ahead = {"fr": lax.rem(fx + n_x - 1, n_x) * NY + y}
    frame_count, patch_count, width = tok_ref.shape
    groups = width // LANES
    patches = q_ref.shape[0]

    def device(g):
        return {"fr": fr - y + g // n_ex, "ex": lax.rem(g, n_ex)}

    def peer(i):
        return lax.rem(me + i * 37, n)

    def device_he(g):
        return {"half": g // n_ex, "ex": lax.rem(g, n_ex)}

    def peer_he(i):
        return lax.rem(me_he + i * 13, n_he)

    loads = []
    for number, (source, target) in enumerate(
        ((up_hbm.at[0], up_ref), (down_hbm.at[0], down_ref), (w_hbm, w_ref))
    ):
        load = pltpu.make_async_copy(source, target, load_sem.at[number])
        load.start()
        loads.append(load)

    barrier = pltpu.get_barrier_semaphore()

    def greet(i, _):
        pl.semaphore_signal(barrier, inc=1, device_id=device(peer(i)), device_id_type=MESH)
        return 0

    def greet_other(i, _):
        other = {"half": lax.rem(half + 1, n_half), "ex": i}
        pl.semaphore_signal(barrier, inc=1, device_id=other, device_id_type=MESH)
        return 0

    lax.fori_loop(0, n_ex, greet_other, 0)
    lax.fori_loop(1, n, greet, 0)
    pl.semaphore_signal(barrier, inc=1, device_id=after, device_id_type=MESH)
    pl.semaphore_signal(barrier, inc=1, device_id=ahead, device_id_type=MESH)

    window_slots = SPE * n_ex
    for f in range(frame_count):
        wide = tok_ref[f].astype(jnp.float32)
        logits = jnp.dot(
            normalize_rows(wide).astype(jnp.bfloat16),
            router_ref[...],
            preferred_element_type=jnp.float32,
        )
        turned = jnp.transpose(logits[:, :LANES])[:window_slots]
        dispatch = jnp.exp(turned - jnp.max(turned, axis=1, keepdims=True))
        dispatch = dispatch / jnp.sum(dispatch, axis=1, keepdims=True)
        data = jnp.dot(
            dispatch.astype(jnp.bfloat16), tok_ref[f], preferred_element_type=jnp.float32
        )
        put_rows(wide_ref, f * window_slots * groups, data)
        slot_ref[f] = (
            wide_ref[f * window_slots * groups : (f + 1) * window_slots * groups]
            .astype(jnp.bfloat16)
            .reshape(slot_ref.shape[1:])
        )
        combine_ref[f] = logits

    mine = pltpu.make_async_copy(slot_ref.at[:, ex], slots_in_ref.at[me_he], own_sem.at[0])
    mine.start()
    pl.semaphore_wait(barrier, n - 1 + n_ex + 2)

    def send_slots(i, _):
        g = peer_he(i)
        pltpu.make_async_remote_copy(
            slot_ref.at[:, lax.rem(g, n_ex)],
            slots_in_ref.at[me_he],
            slot_sem.at[0],
            slot_sem.at[1],
            device_id=device_he(g),
            device_id_type=MESH,
        ).start()
        return 0

    lax.fori_loop(1, n_he, send_slots, 0)
    for f in range(frame_count):
        logits = combine_ref[f]
        combine = jnp.exp(logits - jnp.max(logits, axis=1, keepdims=True))
        combine = combine / jnp.sum(combine, axis=1, keepdims=True)
        combine_ref[f] = combine
    mine.wait()
    rest = slots_in_ref.at[pl.ds(0, n_he - 1)]
    pltpu.make_async_copy(rest, rest, slot_sem.at[1]).wait()
    loads[0].wait()
    loads[1].wait()
    rows = n_he * frame_count * SPE
    wide_ref[: rows * groups] = slots_in_ref[...].reshape(rows * groups, LANES).astype(jnp.float32)
    slot_rows = jnp.concatenate(take_rows(wide_ref, 0, rows, groups, groups), axis=1)
    hidden = jax.nn.gelu(
        jnp.dot(slot_rows.astype(jnp.bfloat16), up_ref[...], preferred_element_type=jnp.float32)
    ).astype(jnp.bfloat16)
    partial_value = jnp.dot(hidden, down_ref[...], preferred_element_type=jnp.float32)
    put_rows(wide_ref, 0, partial_value)
    part_ref[...] = wide_ref[: rows * groups].astype(jnp.bfloat16).reshape(part_ref.shape)
    mine = pltpu.make_async_copy(part_ref.at[me_he], parts_in_ref.at[me_he], own_sem.at[1])
    mine.start()

    def send_parts(i, _):
        g = peer_he(i)
        pltpu.make_async_remote_copy(
            part_ref.at[g],
            parts_in_ref.at[me_he],
            part_sem.at[0],
            part_sem.at[1],
            device_id=device_he(g),
            device_id_type=MESH,
        ).start()
        return 0

    lax.fori_loop(1, n_he, send_parts, 0)
    mine.wait()
    pltpu.make_async_copy(rest, rest, part_sem.at[1]).wait()

    pairs = patch_count // patches
    for f in range(frame_count):
        result = parts_in_ref[:n_ex, f].astype(jnp.float32)
        for h in range(1, n_half):
            result = result + parts_in_ref[h * n_ex : (h + 1) * n_ex, f].astype(jnp.float32)
        wide_ref[: window_slots * groups] = result.reshape(window_slots * groups, LANES)
        result = jnp.concatenate(take_rows(wide_ref, 0, window_slots, groups, groups), axis=1)
        mixture = product(combine_ref[f][:, :window_slots], result)
        normed = normalize_rows(tok_ref[f].astype(jnp.float32) + mixture)
        put_rows(wide_ref, 0, normed)
        packed = wide_ref[: patch_count * groups].reshape(pairs, patches * groups, LANES)
        for p in range(patches):
            x_ref[p, f] = packed[:, p * groups : (p + 1) * groups].astype(jnp.bfloat16)

        def send_tokens(i, _):
            g = peer(i)
            pltpu.make_async_remote_copy(
                x_ref.at[0, f, lax.rem(g, n_ex) * NY + g // n_ex],
                rows_ref.at[0, me, f],
                token_send.at[0],
                token_recv.at[0],
                device_id=device(g),
                device_id_type=MESH,
            ).start()
            return 0

        lax.fori_loop(1, n, send_tokens, 0)
    owns = []
    for p in range(patches):
        mine = pltpu.make_async_copy(
            x_ref.at[p, :, ex * NY + y], rows_ref.at[p, me], own_sem.at[2 + p]
        )
        mine.start()
        owns.append(mine)
        if p == 0:
            continue

        def send_later(i, _):
            g = peer(i)
            pltpu.make_async_remote_copy(
                x_ref.at[p, :, lax.rem(g, n_ex) * NY + g // n_ex],
                rows_ref.at[p, me],
                token_send.at[p],
                token_recv.at[p],
                device_id=device(g),
                device_id_type=MESH,
            ).start()
            return 0

        lax.fori_loop(1, n, send_later, 0)
    loads[2].wait()

    frames = n * frame_count
    pair = 2 * HEAD_SIZE
    all_low = first_lanes((frames, pair))
    low = first_lanes((WINDOW, pair))
    query = lax.broadcasted_iota(jnp.int32, (WINDOW, WINDOW), 0)
    key = lax.broadcasted_iota(jnp.int32, (WINDOW, WINDOW), 1)

    def masks(block):
        start = start_ref[pl.ds(fx * 2 + block, 1), :] - (fx * 2 + block) * WINDOW
        start = jnp.transpose(jnp.broadcast_to(start, (WINDOW, WINDOW)))
        return (key > query) & (key - WINDOW >= start), (key <= query) & (key >= start)

    late, early = masks(1), masks(0)

    def give_back(p, first, last):
        for to in range(first, last):

            @pl.when(y != to)
            def _():
                pltpu.make_async_remote_copy(
                    att_ref.at[p, to],
                    o_ref.at[y, p],
                    back_sem.at[0],
                    back_sem.at[1],
                    device_id={"fr": fr - y + to},
                    device_id_type=MESH,
                ).start()

    for p in range(patches):
        owns[p].wait()
        tokens_in = rows_ref.at[p, pl.ds(0, n - 1)]
        pltpu.make_async_copy(tokens_in, tokens_in, token_recv.at[p]).wait()
        wide_ref[...] = rows_ref[p].reshape(frames * groups, LANES).astype(jnp.float32)
        taken = take_rows(wide_ref, 0, frames, groups, groups)
        inputs = jnp.concatenate([piece.astype(jnp.bfloat16) for piece in taken], axis=1)
        for c in range(2 * WIDTH // 256):
            part = jnp.dot(
                inputs,
                w_ref[:, WIDTH + c * 256 : WIDTH + (c + 1) * 256],
                preferred_element_type=jnp.float32,
            )
            for s in range(2):
                piece = part[:, s * pair : (s + 1) * pair]
                at = c * 256 + s * pair
                if at < WIDTH:
                    piece = normalize_heads(piece, all_low)
                kv_ref[p, :, at : at + pair] = piece.astype(jnp.bfloat16)
        halo = pltpu.make_async_remote_copy(
            kv_ref.at[p, pl.ds(WINDOW, WINDOW)],
            halo_ref.at[p],
            halo_send.at[p],
            halo_recv.at[p],
            device_id=after,
            device_id_type=MESH,
        )
        halo.start()
        for c in range(WIDTH // 256):
            part = jnp.dot(
                inputs, w_ref[:, c * 256 : (c + 1) * 256], preferred_element_type=jnp.float32
            )
            for s in range(2):
                at = c * 256 + s * pair
                q_ref[p, :, at : at + pair] = normalize_heads(
                    part[:, s * pair : (s + 1) * pair], all_low
                )
        attend_block(
            scale_ref,
            late,
            low,
            lambda p, l: q_ref[p, WINDOW:, l],
            lambda p, l: kv_ref[p, :WINDOW, l],
            lambda p, l: kv_ref[p, WINDOW:, l],
            p,
            att_ref,
            NY // 2,
        )
        give_back(p, NY // 2, NY)
        halo.wait()
        attend_block(
            scale_ref,
            early,
            low,
            lambda p, l: q_ref[p, :WINDOW, l],
            lambda p, l: halo_ref[p, :, l],
            lambda p, l: kv_ref[p, :WINDOW, l],
            p,
            att_ref,
            0,
        )
        give_back(p, 0, NY // 2)
    mine = pltpu.make_async_copy(att_ref.at[:, y], o_ref.at[y], own_sem.at[2 + patches])
    mine.start()
    mine.wait()
    pltpu.make_async_copy(rest, rest, slot_sem.at[0]).wait()
    pltpu.make_async_copy(rest, rest, part_sem.at[0]).wait()
    for p in range(patches):
        tokens_in = rows_ref.at[p, pl.ds(0, n - 1)]
        pltpu.make_async_copy(tokens_in, tokens_in, token_send.at[p]).wait()
    back = o_ref.at[pl.ds(0, NY - 1)]
    pltpu.make_async_copy(back, back, back_sem.at[1]).wait()
    pltpu.make_async_copy(back, back, back_sem.at[0]).wait()


def local(
    frame_patch_tokens,
    episode_first_frame,
    router,
    expert_up_weight,
    expert_down_weight,
    query_key_value_weight,
    head_score_scale,
):
    tokens = frame_patch_tokens[0, 0]
    frame_count, patch_count, width = tokens.shape
    n_ex = lax.axis_size("ex")
    n_half = lax.axis_size("half")
    n_he = n_half * n_ex
    n = NY * n_ex
    frames = n * frame_count
    span = frames // NY
    patches = patch_count // n
    groups = width // LANES
    slots = SPE * n_ex
    hidden = expert_up_weight.shape[2]
    starts = episode_first_frame.reshape(-1, WINDOW)
    vmem = pl.BlockSpec(memory_space=pltpu.VMEM)
    hbm = pl.BlockSpec(memory_space=pl.ANY)
    dma = pltpu.SemaphoreType.DMA

    def held(*shape):
        return pltpu.VMEM(shape, jnp.bfloat16)

    back = pl.pallas_call(
        functools.partial(whole_kernel, n_half, n_ex),
        out_shape=jax.ShapeDtypeStruct((NY, patches, span, WIDTH), jnp.bfloat16),
        in_specs=[pl.BlockSpec(memory_space=pltpu.SMEM), vmem, vmem, vmem, hbm, hbm, hbm],
        out_specs=vmem,
        scratch_shapes=[
            held(frame_count, n_ex, SPE * groups, LANES),
            held(n_he, frame_count, SPE * groups, LANES),
            held(n_he, frame_count, SPE * groups, LANES),
            held(n_he, frame_count, SPE * groups, LANES),
            pltpu.VMEM((frame_count, patch_count, router.shape[1]), jnp.float32),
            held(patches, frame_count, n, groups, LANES),
            held(patches, n, frame_count, groups, LANES),
            pltpu.VMEM((frames * groups, LANES), jnp.float32),
            held(width, hidden),
            held(hidden, width),
            held(*query_key_value_weight.shape),
            held(patches, frames, WIDTH),
            held(patches, frames, 2 * WIDTH),
            held(patches, WINDOW, 2 * WIDTH),
            held(patches, NY, span, WIDTH),
            dma((3,)),
            dma((3 + patches,)),
            dma((2,)),
            dma((2,)),
            dma((patches,)),
            dma((patches,)),
            dma((patches,)),
            dma((patches,)),
            dma((2,)),
        ],
        compiler_params=pltpu.CompilerParams(collective_id=0, has_side_effects=True),
        name="whole",
    )(
        head_score_scale,
        starts,
        tokens,
        router,
        expert_up_weight,
        expert_down_weight,
        query_key_value_weight,
    )
    return back.transpose(2, 0, 1, 3).reshape(1, span, NY * patches, WIDTH)


def solution(mesh):
    placed = (
        P("half", "fr", "ex", None, None),
        P("half", None),
        P(),
        P("ex", None, "half"),
        P("ex", "half", None),
        P(),
        P(),
    )
    return jax.shard_map(
        local, mesh=mesh, in_specs=placed, out_specs=P("half", "fr", "ex", None), check_vma=False
    )
```

```python
import functools
import math

import jax
import jax.numpy as jnp
from jax import lax
from jax.experimental import pallas as pl
from jax.experimental.pallas import tpu as pltpu
from jax.sharding import PartitionSpec as P

SPE = 2
HEAD_SIZE = 64
HEADS = 8
WIDTH = HEADS * HEAD_SIZE
NY = 8
WINDOW = 128
LANES = 128
MESH = pl.DeviceIdType.MESH

epsilon = 1e-06


def normalize_rows(values):
    return values * lax.rsqrt(jnp.mean(values * values, axis=-1, keepdims=True) + epsilon)


def first_lanes(shape):
    lane = lax.broadcasted_iota(jnp.int32, shape, len(shape) - 1)
    return lax.rem(lane, 2 * HEAD_SIZE) < HEAD_SIZE


def normalize_heads(values, low):
    square = values * values
    low_sum = jnp.sum(jnp.where(low, square, 0.0), axis=-1, keepdims=True)
    high_sum = jnp.sum(jnp.where(low, 0.0, square), axis=-1, keepdims=True)
    scale = jnp.where(
        low,
        lax.rsqrt(low_sum * (1.0 / HEAD_SIZE) + epsilon),
        lax.rsqrt(high_sum * (1.0 / HEAD_SIZE) + epsilon),
    )
    return (values * scale).astype(jnp.bfloat16)


def attend_block(scale_ref, allowed, low, q, before, own, p, out_ref, y0, enter, leave):
    pair = 2 * HEAD_SIZE
    contract = (((1,), (1,)), ((), ()))
    for c in range(WIDTH // pair):
        lanes = slice(c * pair, (c + 1) * pair)
        keys = slice(2 * c * pair, (2 * c + 1) * pair)
        values = slice((2 * c + 1) * pair, (2 * c + 2) * pair)
        enter(c)
        queries = q(p, lanes)
        outs, scales = [], []
        for side in range(2):
            picked = jnp.where(low if side == 0 else ~low, queries, jnp.zeros_like(queries))
            factor = scale_ref[2 * c + side] * (1.0 / math.sqrt(HEAD_SIZE))
            total = None
            out = None
            for kv, mask in zip((before, own), allowed):
                score = lax.dot_general(
                    picked, kv(p, keys), contract, preferred_element_type=jnp.float32
                )
                weight = jnp.where(mask, jnp.exp(score * factor), 0.0)
                part_total = jnp.sum(weight, axis=-1, keepdims=True)
                part = jnp.dot(
                    weight.astype(jnp.bfloat16), kv(p, values), preferred_element_type=jnp.float32
                )
                total = part_total if total is None else total + part_total
                out = part if out is None else out + part
            outs.append(out)
            scales.append(1.0 / total)
        result = jnp.where(low, outs[0], outs[1]) * jnp.where(low, scales[0], scales[1])
        result = result.astype(out_ref.dtype)
        span = out_ref.shape[2]
        for y in range(WINDOW // span):
            out_ref[p, y0 + y, :, lanes] = result[y * span : (y + 1) * span]
        leave(c)


def split(values):
    first = values.astype(jnp.bfloat16)
    rest = values - first.astype(jnp.float32)
    second = rest.astype(jnp.bfloat16)
    third = (rest - second.astype(jnp.float32)).astype(jnp.bfloat16)
    return first, second, third


def product(left, right):
    a, b, c = split(left)
    x, y, z = split(right)
    return jnp.dot(
        jnp.concatenate([a, a, b, b, a, c], axis=1),
        jnp.concatenate([x, y, x, y, z, x], axis=0),
        preferred_element_type=jnp.float32,
    )


def put_rows(wide_ref, first, values):
    rows, width = values.shape
    groups = width // LANES
    for k in range(groups):
        wide_ref[pl.ds(first + k, rows, stride=groups), :] = values[:, k * LANES : (k + 1) * LANES]


def take_rows(wide_ref, first, rows, stride, groups):
    return [wide_ref[pl.ds(first + k, rows, stride=stride), :] for k in range(groups)]


def whole_kernel(
    n_half,
    n_ex,
    scale_ref,
    start_ref,
    tok_hbm,
    router_hbm,
    up_hbm,
    down_hbm,
    w_hbm,
    o_ref,
    tok_ref,
    router_ref,
    slot_ref,
    slots_in_ref,
    part_ref,
    parts_in_ref,
    combine_ref,
    x_ref,
    rows_ref,
    wide_ref,
    up_ref,
    down_ref,
    w_ref,
    q_ref,
    kv_ref,
    halo_ref,
    att_ref,
    load_sem,
    own_sem,
    slot_sem,
    part_sem,
    token_send,
    token_recv,
    halo_send,
    halo_recv,
    back_sem,
):
    half = lax.axis_index("half")
    ex = lax.axis_index("ex")
    fr = lax.axis_index("fr")
    fx = fr // NY
    y = lax.rem(fr, NY)
    n = NY * n_ex
    n_x = lax.axis_size("fr") // NY
    me = y * n_ex + ex
    n_he = n_half * n_ex
    me_he = half * n_ex + ex
    after = {"fr": lax.rem(fx + 1, n_x) * NY + y}
    ahead = {"fr": lax.rem(fx + n_x - 1, n_x) * NY + y}
    frame_count, patch_count, width = tok_ref.shape
    groups = width // LANES
    patches = q_ref.shape[0]

    ys = [lax.rem(y + d, NY) for d in range(NY)]
    frs = [fr - y + to for to in ys]
    other = lax.rem(half + 1, n_half)
    pair = 2 * HEAD_SIZE
    head_pairs = WIDTH // pair

    def turn(i):
        return lax.rem(ex + i * 5, n_ex)

    barrier = pltpu.get_barrier_semaphore()

    def signal(device):
        pl.semaphore_signal(barrier, inc=1, device_id=device, device_id_type=MESH)

    signal({"half": other})
    for d in range(1, NY):
        signal({"fr": frs[d]})
    signal(after)
    signal(ahead)

    def greet(i, _):
        e = turn(i)
        signal({"half": other, "ex": e})
        for d in range(NY):
            signal({"fr": frs[d], "ex": e})
        return 0

    first_loads = [
        pltpu.make_async_copy(tok_hbm.at[0, 0], tok_ref, load_sem.at[0]),
        pltpu.make_async_copy(router_hbm, router_ref, load_sem.at[1]),
    ]
    loads = [
        pltpu.make_async_copy(up_hbm.at[0], up_ref, load_sem.at[2]),
        pltpu.make_async_copy(down_hbm.at[0], down_ref, load_sem.at[3]),
    ]
    for load in first_loads:
        load.start()
    lax.fori_loop(1, n_ex, greet, 0)
    for load in loads:
        load.start()
    for c in range(head_pairs):
        for part, at in ((1, 2 * c), (2, 2 * c + 1), (0, 2 * head_pairs + c)):
            pltpu.make_async_copy(
                w_hbm.at[:, pl.ds(part * WIDTH + c * pair, pair)],
                w_ref.at[:, pl.ds(at * pair, pair)],
                load_sem.at[4],
            ).start()
    for load in first_loads:
        load.wait()

    window_slots = SPE * n_ex
    block = window_slots * groups

    def send_all(pick, place, sems, f):
        def one(h, e):
            device = {"half": h, "ex": e}
            pltpu.make_async_remote_copy(
                pick(h, e),
                place,
                sems.at[0, f],
                sems.at[1, f],
                device_id=device,
                device_id_type=MESH,
            ).start()

        def step(i, _):
            e = turn(i)
            one(other, e)
            one(half, e)
            return 0

        one(other, ex)
        lax.fori_loop(1, n_ex, step, 0)

    slot_owns = []
    for f in range(frame_count):
        wide = tok_ref[f].astype(jnp.float32)
        logits = jnp.dot(
            normalize_rows(wide).astype(jnp.bfloat16),
            router_ref[...],
            preferred_element_type=jnp.float32,
        )
        turned = jnp.transpose(logits[:, :LANES])[:window_slots]
        dispatch = jnp.exp(turned - jnp.max(turned, axis=1, keepdims=True))
        dispatch = dispatch / jnp.sum(dispatch, axis=1, keepdims=True)
        data = jnp.dot(
            dispatch.astype(jnp.bfloat16), tok_ref[f], preferred_element_type=jnp.float32
        )
        put_rows(wide_ref, f * block, data)
        slot_ref[f] = (
            wide_ref[f * block : (f + 1) * block]
            .astype(jnp.bfloat16)
            .reshape(slot_ref.shape[1:])
        )
        if f == 0:
            pl.semaphore_wait(barrier, n - 1 + n_ex + 2)
        mine = pltpu.make_async_copy(slot_ref.at[f, ex], slots_in_ref.at[f, me_he], own_sem.at[f])
        mine.start()
        slot_owns.append(mine)
        send_all(lambda h, e: slot_ref.at[f, e], slots_in_ref.at[f, me_he], slot_sem, f)
        combine = jnp.exp(logits - jnp.max(logits, axis=1, keepdims=True))
        combine_ref[f] = combine / jnp.sum(combine, axis=1, keepdims=True)

    rows = n_he * SPE
    part_owns = []
    for f in range(frame_count):
        slot_owns[f].wait()
        rest = slots_in_ref.at[f, pl.ds(0, n_he - 1)]
        pltpu.make_async_copy(rest, rest, slot_sem.at[1, f]).wait()
        if f == 0:
            loads[0].wait()
            loads[1].wait()
        wide_ref[: rows * groups] = (
            slots_in_ref[f].reshape(rows * groups, LANES).astype(jnp.float32)
        )
        slot_rows = jnp.concatenate(take_rows(wide_ref, 0, rows, groups, groups), axis=1)
        hidden = jax.nn.gelu(
            jnp.dot(slot_rows.astype(jnp.bfloat16), up_ref[...], preferred_element_type=jnp.float32)
        ).astype(jnp.bfloat16)
        partial_value = jnp.dot(hidden, down_ref[...], preferred_element_type=jnp.float32)
        put_rows(wide_ref, 0, partial_value)
        part_ref[f] = (
            wide_ref[: rows * groups].astype(jnp.bfloat16).reshape(part_ref.shape[1:])
        )
        mine = pltpu.make_async_copy(
            part_ref.at[f, me_he], parts_in_ref.at[f, me_he], own_sem.at[frame_count + f]
        )
        mine.start()
        part_owns.append(mine)
        send_all(
            lambda h, e: part_ref.at[f, h * n_ex + e], parts_in_ref.at[f, me_he], part_sem, f
        )

    pairs = patch_count // patches

    def send_group(pick, place, p):
        def one(d, e):
            pltpu.make_async_remote_copy(
                pick(e * NY + ys[d]),
                place,
                token_send.at[p],
                token_recv.at[p],
                device_id={"fr": frs[d], "ex": e},
                device_id_type=MESH,
            ).start()

        def step(i, _):
            e = turn(i)
            for d in range(NY):
                one(d, e)
            return 0

        for d in range(1, NY):
            one(d, ex)
        lax.fori_loop(1, n_ex, step, 0)

    for f in range(frame_count):
        part_owns[f].wait()
        rest = parts_in_ref.at[f, pl.ds(0, n_he - 1)]
        pltpu.make_async_copy(rest, rest, part_sem.at[1, f]).wait()
        result = parts_in_ref[f, :n_ex].astype(jnp.float32)
        for h in range(1, n_half):
            result = result + parts_in_ref[f, h * n_ex : (h + 1) * n_ex].astype(jnp.float32)
        wide_ref[: window_slots * groups] = result.reshape(window_slots * groups, LANES)
        result = jnp.concatenate(take_rows(wide_ref, 0, window_slots, groups, groups), axis=1)
        mixture = product(combine_ref[f][:, :window_slots], result)
        normed = normalize_rows(tok_ref[f].astype(jnp.float32) + mixture)
        put_rows(wide_ref, 0, normed)
        packed = wide_ref[: patch_count * groups].reshape(pairs, patches * groups, LANES)
        for p in range(patches):
            x_ref[p, f] = packed[:, p * groups : (p + 1) * groups].astype(jnp.bfloat16)

        send_group(lambda at: x_ref.at[0, f, at], rows_ref.at[0, me, f], 0)
    owns = []
    for p in range(patches):
        mine = pltpu.make_async_copy(
            x_ref.at[p, :, ex * NY + y], rows_ref.at[p, me], own_sem.at[2 * frame_count + p]
        )
        mine.start()
        owns.append(mine)
        if p == 0:
            continue

        send_group(lambda at: x_ref.at[p, :, at], rows_ref.at[p, me], p)
    pltpu.make_async_copy(w_ref, w_ref, load_sem.at[4]).wait()

    frames = n * frame_count
    all_low = first_lanes((frames, pair))
    low = first_lanes((WINDOW, pair))
    query = lax.broadcasted_iota(jnp.int32, (WINDOW, WINDOW), 0)
    key = lax.broadcasted_iota(jnp.int32, (WINDOW, WINDOW), 1)

    def masks(block):
        start = start_ref[pl.ds(fx * 2 + block, 1), :] - (fx * 2 + block) * WINDOW
        start = jnp.transpose(jnp.broadcast_to(start, (WINDOW, WINDOW)))
        return (key > query) & (key - WINDOW >= start), (key <= query) & (key >= start)

    late, early = masks(1), masks(0)

    def give_back(p, first, last, at, lanes):
        for to in range(first, last):

            @pl.when(y != to)
            def _():
                pltpu.make_async_remote_copy(
                    att_ref.at[p, to, :, pl.ds(at, lanes)],
                    o_ref.at[y, p, :, pl.ds(at, lanes)],
                    back_sem.at[0],
                    back_sem.at[1],
                    device_id={"fr": fr - y + to},
                    device_id_type=MESH,
                ).start()

    for p in range(patches):
        owns[p].wait()
        tokens_in = rows_ref.at[p, pl.ds(0, n - 1)]
        pltpu.make_async_copy(tokens_in, tokens_in, token_recv.at[p]).wait()
        wide_ref[...] = rows_ref[p].reshape(frames * groups, LANES).astype(jnp.float32)
        taken = take_rows(wide_ref, 0, frames, groups, groups)
        inputs = jnp.concatenate([piece.astype(jnp.bfloat16) for piece in taken], axis=1)
        halos = []
        for c in range(head_pairs):
            lanes = slice(2 * c * pair, (2 * c + 2) * pair)
            part = jnp.dot(inputs, w_ref[:, lanes], preferred_element_type=jnp.float32)
            kv_ref[p, :, 2 * c * pair : (2 * c + 1) * pair] = normalize_heads(
                part[:, :pair], all_low
            )
            kv_ref[p, :, (2 * c + 1) * pair : (2 * c + 2) * pair] = part[:, pair:].astype(
                jnp.bfloat16
            )
            halo = pltpu.make_async_remote_copy(
                kv_ref.at[p, pl.ds(WINDOW, WINDOW), pl.ds(2 * c * pair, 2 * pair)],
                halo_ref.at[p, :, pl.ds(2 * c * pair, 2 * pair)],
                halo_send.at[p, c],
                halo_recv.at[p, c],
                device_id=after,
                device_id_type=MESH,
            )
            halo.start()
            halos.append(halo)
        for c in range(WIDTH // 256):
            at = 2 * WIDTH + c * 256
            part = jnp.dot(inputs, w_ref[:, at : at + 256], preferred_element_type=jnp.float32)
            for s in range(2):
                at = c * 256 + s * pair
                q_ref[p, :, at : at + pair] = normalize_heads(
                    part[:, s * pair : (s + 1) * pair], all_low
                )
        attend_block(
            scale_ref,
            late,
            low,
            lambda p, l: q_ref[p, WINDOW:, l],
            lambda p, l: kv_ref[p, :WINDOW, l],
            lambda p, l: kv_ref[p, WINDOW:, l],
            p,
            att_ref,
            NY // 2,
            lambda c: None,
            lambda c: None,
        )
        give_back(p, NY // 2, NY, 0, WIDTH)
        attend_block(
            scale_ref,
            early,
            low,
            lambda p, l: q_ref[p, :WINDOW, l],
            lambda p, l: halo_ref[p, :, l],
            lambda p, l: kv_ref[p, :WINDOW, l],
            p,
            att_ref,
            0,
            lambda c: halos[c].wait(),
            lambda c: give_back(p, 0, NY // 2, c * pair, pair),
        )
    mine = pltpu.make_async_copy(att_ref.at[:, y], o_ref.at[y], own_sem.at[2 * frame_count + patches])
    mine.start()
    mine.wait()
    for f in range(frame_count):
        rest = slots_in_ref.at[f, pl.ds(0, n_he - 1)]
        pltpu.make_async_copy(rest, rest, slot_sem.at[0, f]).wait()
        pltpu.make_async_copy(rest, rest, part_sem.at[0, f]).wait()
    for p in range(patches):
        tokens_in = rows_ref.at[p, pl.ds(0, n - 1)]
        pltpu.make_async_copy(tokens_in, tokens_in, token_send.at[p]).wait()
    back = o_ref.at[pl.ds(0, NY - 1)]
    pltpu.make_async_copy(back, back, back_sem.at[1]).wait()
    pltpu.make_async_copy(back, back, back_sem.at[0]).wait()


def local(
    frame_patch_tokens,
    episode_first_frame,
    router,
    expert_up_weight,
    expert_down_weight,
    query_key_value_weight,
    head_score_scale,
):
    tokens = frame_patch_tokens.shape[2:]
    frame_count, patch_count, width = tokens
    n_ex = lax.axis_size("ex")
    n_half = lax.axis_size("half")
    n_he = n_half * n_ex
    n = NY * n_ex
    frames = n * frame_count
    span = frames // NY
    patches = patch_count // n
    groups = width // LANES
    slots = SPE * n_ex
    hidden = expert_up_weight.shape[2]
    starts = episode_first_frame.reshape(-1, WINDOW)
    vmem = pl.BlockSpec(memory_space=pltpu.VMEM)
    hbm = pl.BlockSpec(memory_space=pl.ANY)
    dma = pltpu.SemaphoreType.DMA

    def held(*shape):
        return pltpu.VMEM(shape, jnp.bfloat16)

    back = pl.pallas_call(
        functools.partial(whole_kernel, n_half, n_ex),
        out_shape=jax.ShapeDtypeStruct((NY, patches, span, WIDTH), jnp.bfloat16),
        in_specs=[pl.BlockSpec(memory_space=pltpu.SMEM), vmem] + [hbm] * 5,
        out_specs=vmem,
        scratch_shapes=[
            held(*tokens),
            held(*router.shape),
            held(frame_count, n_ex, SPE * groups, LANES),
            held(frame_count, n_he, SPE * groups, LANES),
            held(frame_count, n_he, SPE * groups, LANES),
            held(frame_count, n_he, SPE * groups, LANES),
            pltpu.VMEM((frame_count, patch_count, router.shape[1]), jnp.float32),
            held(patches, frame_count, n, groups, LANES),
            held(patches, n, frame_count, groups, LANES),
            pltpu.VMEM((frames * groups, LANES), jnp.float32),
            held(width, hidden),
            held(hidden, width),
            held(*query_key_value_weight.shape),
            held(patches, frames, WIDTH),
            held(patches, frames, 2 * WIDTH),
            held(patches, WINDOW, 2 * WIDTH),
            held(patches, NY, span, WIDTH),
            dma((5,)),
            dma((2 * frame_count + patches + 1,)),
            dma((2, frame_count)),
            dma((2, frame_count)),
            dma((patches,)),
            dma((patches,)),
            dma((patches, WIDTH // (2 * HEAD_SIZE))),
            dma((patches, WIDTH // (2 * HEAD_SIZE))),
            dma((2,)),
        ],
        compiler_params=pltpu.CompilerParams(collective_id=0, has_side_effects=True),
        name="whole",
    )(
        head_score_scale,
        starts,
        frame_patch_tokens,
        router,
        expert_up_weight,
        expert_down_weight,
        query_key_value_weight,
    )
    return back.transpose(2, 0, 1, 3).reshape(1, span, NY * patches, WIDTH)


def solution(mesh):
    placed = (
        P("half", "fr", "ex", None, None),
        P("half", None),
        P(),
        P("ex", None, "half"),
        P("ex", "half", None),
        P(),
        P(),
    )
    return jax.shard_map(
        local, mesh=mesh, in_specs=placed, out_specs=P("half", "fr", "ex", None), check_vma=False
    )
```
